32 devices in a mesh: dp: 2 (over core), row: 8 (over z, y), col: 2 (over x).
Axes of the slice: x: 2, y: 2, z: 4, core: 2. Of those that a mesh axis runs over, the one named last changes fastest.
Arguments:
- inputs: bfloat16 [8192, 1280], P(('dp', 'row'), 'col'), may hold values from -6 to 6
- input_weight: bfloat16 [1280, 3, 1280], P('col', None, 'row'), may hold values from -0.15625 to 0.15625
- output_weight: bfloat16 [1280, 1280], P('row', 'col'), may hold values from -2 to 2
- up_weight: bfloat16 [1280, 1280], P('col', 'row'), may hold values from -0.15625 to 0.15625
- down_weight: bfloat16 [1280, 1280], P('row', 'col'), may hold values from -0.15625 to 0.15625
- attend_gain: float32 [1280], P('col'), may hold values from 0.5 to 2
- feed_gain: float32 [1280], P('col'), may hold values from 0.5 to 2
- query_gain: float32 [80], replicated, may hold values from 0.6 to 1.8
- branch_points: int32 [4, 8], P(('dp', 'col')), may hold values from 128 to 1024
- cotangent: bfloat16 [8192, 1280], P(('dp', 'row'), 'col'), may hold values from -6 to 6
Outputs:
- output: bfloat16 [8192, 1280], P(('dp', 'row'), 'col')
- input_grad: float32 [8192, 1280], P(('dp', 'row'), 'col')
- input_weight_grad: float32 [1280, 3, 1280], P('col', None, 'row')
- output_weight_grad: float32 [1280, 1280], P('row', 'col')
- up_weight_grad: float32 [1280, 1280], P('col', 'row')
- down_weight_grad: float32 [1280, 1280], P('row', 'col')
- attend_gain_grad: float32 [1280], P('col')
- feed_gain_grad: float32 [1280], P('col')
- query_gain_grad: float32 [80], replicated
- rms_stats: float32 [3, 8192], P(None, ('dp', 'row'))
The draws below stay inside these ranges and needn't reach their ends.
Inputs may be any that keep to these rules, and one draw needn't show every extreme that they name: Continuation j of group g reads the first branch_points[g, j] patches of its own prompt.
All inputs are finite; a program needn't handle non-finite values.
Results may differ from the reference program's by a relative error of at most 0.014.
Values may be sent and summed in bfloat16 or wider, within the bound.
No kernel may reach another device: no remote copies, remote signals or barrier semaphores. Data moves between devices by JAX's collectives and lax.ppermute only.
A program may use at most 192 MiB of HBM per device.

```python
import math
import jax
import jax.numpy as jnp
from jax import lax

D = 1280
HEADS = 16
HEAD_DIM = 80
FF = 1280
PROMPT = 1024
CONT_LEN = 128
N_CONT = 8
GROUP_LEN = 2048
GROUPS = 4
TOKENS = 8192


def plant(drawn, key, low, largest):
    dims = drawn.shape
    spot = [jax.random.randint(jax.random.fold_in(key, axis), (), 0, dims[axis]) for axis in range(len(dims))]
    drawn = drawn.at[tuple(spot)].set(low)
    longest = dims.index(max(dims))
    spot[longest] = (spot[longest] + 1) % dims[longest]
    return drawn.at[tuple(spot)].set(largest)


def levels(rng, shape, split, least, high):
    gain = 1.0
    for dim, blocks in split:
        draws = jax.random.uniform(jax.random.fold_in(jax.random.fold_in(rng, 6), dim), (blocks,), jnp.float32, least / len(split), high / len(split))
        gain = gain * jnp.repeat(jnp.exp(draws), shape[dim] // blocks).reshape((-1,) + (1,) * (len(shape) - 1 - dim))
    return gain


def normal_values(stream_key, extent, spread, bound, split=(), dtype=jnp.bfloat16):
    array = jax.random.normal(stream_key, extent, jnp.float32) * spread
    if len(split) > 0:
        array = levels(stream_key, extent, split, -0.22, 0.18) * array
    return jnp.clip(array, min=-bound, max=bound).astype(dtype)


def setup_inputs(seed: int = 0) -> dict:
    splits = jax.random.split(jax.random.key(seed), 11)
    inputs = normal_values(splits[0], (TOKENS, D), 1.0, 6.0, ((0, 16), (1, 2)))
    input_weight = normal_values(splits[1], (D, 3, HEADS * HEAD_DIM), D ** -0.5, 0.15625, ((0, 2), (2, 8)))
    output_weight = normal_values(splits[2], (HEADS * HEAD_DIM, D), (HEADS * HEAD_DIM * 8 // PROMPT) ** -0.5, 2.0, ((0, 8), (1, 2)))
    up_weight = normal_values(splits[3], (D, FF), D ** -0.5, 0.15625, ((0, 2), (1, 8)))
    down_weight = normal_values(splits[4], (FF, D), FF ** -0.5, 0.15625, ((0, 8), (1, 2)))
    attend_gain = jnp.clip(jnp.exp(math.log(2.0) - 1.3862944 * jax.random.uniform(splits[5], (D,), jnp.float32) ** levels(splits[5], (D,), ((0, 2),), -0.2, 0.2)), 0.5, 2.0)
    feed_gain = jnp.clip(jnp.exp(math.log(2.0) - 1.3862944 * jax.random.uniform(splits[6], (D,), jnp.float32) ** levels(splits[6], (D,), ((0, 2),), -0.2, 0.2)), 0.5, 2.0)
    query_gain = jnp.clip(jnp.exp(jax.random.uniform(splits[7], (HEAD_DIM,), jnp.float32, math.log(0.6), math.log(1.8))), 0.6, 1.8)
    branch_points = plant(jax.random.randint(splits[8], (GROUPS, N_CONT), PROMPT // 8, PROMPT + 1), jax.random.fold_in(splits[8], 1), PROMPT // 8, PROMPT).astype(jnp.int32)
    cotangent = normal_values(splits[9], (TOKENS, D), 1.0, 6.0, ((0, 16), (1, 2)))
    return dict(inputs=inputs, input_weight=input_weight, output_weight=output_weight, up_weight=up_weight, down_weight=down_weight, attend_gain=attend_gain, feed_gain=feed_gain, query_gain=query_gain, branch_points=branch_points, cotangent=cotangent)


EPS = 1e-06
NEG = -1e+30
HIGH = lax.Precision.HIGHEST

@jax.custom_vjp
def low(v):
    return lax.optimization_barrier(v.astype(jnp.bfloat16)).astype(jnp.float32)

@jax.custom_vjp
def low_back(v):
    return v

def low_keep(v):
    return (low(v), None)

def low_pass(kept, grad):
    return (grad,)

def back_keep(v):
    return (v, None)

def back_low(kept, grad):
    return (low(grad),)
low.defvjp(low_keep, low_pass)
low_back.defvjp(back_keep, back_low)

def softmax_rows(scores):
    shifted = jnp.exp(scores - lax.optimization_barrier(jnp.max(scores, axis=-1, keepdims=True)))
    return shifted / lax.optimization_barrier(jnp.sum(shifted, axis=-1, keepdims=True))

def group_attend(args):
    q_all, k_all, v_all, offsets = args
    rows = jnp.arange(PROMPT).astype(jnp.int32)
    causal_p = rows[None, :] <= rows[:, None]
    reach = rows[None, None, :] < offsets.astype(jnp.int32)[:, None, None]
    inner = jnp.arange(CONT_LEN).astype(jnp.int32)
    causal_c = inner[None, :] <= inner[:, None]
    query_p = q_all[:PROMPT]
    query_c = q_all[PROMPT:].reshape(N_CONT, CONT_LEN, HEADS, HEAD_DIM)
    keys_p = k_all[:PROMPT]
    keys_c = k_all[PROMPT:].reshape(N_CONT, CONT_LEN, HEADS, HEAD_DIM)
    vals_p = v_all[:PROMPT]
    vals_c = v_all[PROMPT:].reshape(N_CONT, CONT_LEN, HEADS, HEAD_DIM)
    score_pp = low_back(jnp.einsum('qhd,khd->hqk', query_p, keys_p, precision=HIGH))
    score_cp = low_back(jnp.einsum('nqhd,khd->hnqk', query_c, keys_p, precision=HIGH))
    score_cc = low_back(jnp.einsum('nqhd,nkhd->hnqk', query_c, keys_c, precision=HIGH))
    score_pp = jnp.where(causal_p, score_pp, NEG)
    score_cp = jnp.where(reach[None], score_cp, NEG)
    score_cc = jnp.where(causal_c, score_cc, NEG)
    prob_pp = low(softmax_rows(score_pp))
    prob_c = low(softmax_rows(jnp.concatenate([score_cp, score_cc], axis=-1)))
    prob_cp = prob_c[..., :PROMPT]
    prob_cc = prob_c[..., PROMPT:]
    out_p = jnp.einsum('hqk,khd->qhd', prob_pp, vals_p, precision=HIGH)
    out_c = jnp.einsum('hnqk,khd->nqhd', prob_cp, vals_p, precision=HIGH)
    out_c = out_c + jnp.einsum('hnqk,nkhd->nqhd', prob_cc, vals_c, precision=HIGH)
    return jnp.concatenate([out_p, out_c.reshape(N_CONT * CONT_LEN, HEADS, HEAD_DIM)], axis=0)

def layer(resid, input_weight, output_weight, up_weight, down_weight, attend_gain, feed_gain, query_gain, offsets):
    inv_one = lax.rsqrt(lax.optimization_barrier(jnp.mean(resid * resid, axis=-1, keepdims=True)) + EPS)
    normed_one = low(resid * inv_one * attend_gain)
    qkv = jnp.dot(normed_one, input_weight.reshape(D, 3 * HEADS * HEAD_DIM), precision=HIGH)
    qkv = low_back(qkv).reshape(GROUPS, GROUP_LEN, 3, HEADS, HEAD_DIM)
    q_low = low(qkv[:, :, 0] * (query_gain / math.sqrt(HEAD_DIM)))
    k_low = low(qkv[:, :, 1])
    v_low = low(qkv[:, :, 2])
    attended = lax.map(jax.checkpoint(group_attend), (q_low, k_low, v_low, offsets))
    attended = low(low_back(attended)).reshape(TOKENS, HEADS * HEAD_DIM)
    attn_branch = low_back(jnp.dot(attended, output_weight, precision=HIGH))
    hidden = resid + attn_branch
    inv_two = lax.rsqrt(lax.optimization_barrier(jnp.mean(hidden * hidden, axis=-1, keepdims=True)) + EPS)
    normed_two = low(hidden * inv_two * feed_gain)
    pre = low_back(jnp.dot(normed_two, up_weight, precision=HIGH))
    act = low(jax.nn.silu(pre))
    feed_branch = low_back(jnp.dot(act, down_weight, precision=HIGH))
    stream = hidden + feed_branch
    return (stream, (attn_branch, feed_branch))

def reference(inputs, input_weight, output_weight, up_weight, down_weight, attend_gain, feed_gain, query_gain, branch_points, cotangent):
    primals = (inputs.astype(jnp.float32), input_weight.astype(jnp.float32), output_weight.astype(jnp.float32), up_weight.astype(jnp.float32), down_weight.astype(jnp.float32), attend_gain.astype(jnp.float32), feed_gain.astype(jnp.float32), query_gain.astype(jnp.float32))

    def run(resid, w_in, w_out, w_up, w_down, gain_a, gain_f, gain_q):
        return layer(resid, w_in, w_out, w_up, w_down, gain_a, gain_f, gain_q, branch_points)
    stream, pull, extras = jax.vjp(run, *primals, has_aux=True)
    grads = pull(cotangent.astype(jnp.float32))
    attn_branch, feed_branch = extras
    rms_stats = jnp.stack([jnp.sqrt(lax.optimization_barrier(jnp.mean(attn_branch * attn_branch, axis=-1))), jnp.sqrt(lax.optimization_barrier(jnp.mean(feed_branch * feed_branch, axis=-1))), jnp.sqrt(lax.optimization_barrier(jnp.mean(stream * stream, axis=-1)))])
    return (stream.astype(jnp.bfloat16), grads[0], grads[1], grads[2], grads[3], grads[4], grads[5], grads[6], grads[7], rms_stats)
```

```python
import math

import jax
import jax.numpy as jnp
from jax import lax
from jax.sharding import Mesh, PartitionSpec as P

PROMPT = 1024
CONT_LEN = 128
N_CONT = 8
GROUP_LEN = PROMPT + N_CONT * CONT_LEN
EPS = 1e-06
NEG = -1e30
F32 = jnp.float32
BF16 = jnp.bfloat16


def xch(a, axis):
    return lax.ppermute(a, axis, [(0, 1), (1, 0)])


def swap(a):
    return lax.ppermute(a, ("k", "l"), [(0, 0), (1, 2), (2, 1), (3, 3)])


def place(pieces, count):
    out = jnp.zeros((count,) + pieces[0][1].shape, pieces[0][1].dtype)
    for index, piece in pieces:
        out = lax.dynamic_update_index_in_dim(out, piece, index, 0)
    return out


def pick(a, index, axis=0):
    return lax.dynamic_index_in_dim(a, index, axis, keepdims=False)


def dot(a, b, ca, cb):
    return lax.dot_general(a, b, (((ca,), (cb,)), ((), ())), preferred_element_type=F32)


def split_group(values):
    heads, head_dim = (values.shape[1], values.shape[2])
    return (values[:PROMPT], values[PROMPT:].reshape(N_CONT, CONT_LEN, heads, head_dim))


def join_group(prompt_part, cont_part):
    heads, head_dim = (prompt_part.shape[1], prompt_part.shape[2])
    return jnp.concatenate(
        [prompt_part, cont_part.reshape(N_CONT * CONT_LEN, heads, head_dim)], axis=0
    )


def score_blocks(q_all, k_all, offsets):
    query_p, query_c = split_group(q_all)
    keys_p, keys_c = split_group(k_all)
    rows = jnp.arange(PROMPT, dtype=jnp.int32)
    inner = jnp.arange(CONT_LEN, dtype=jnp.int32)
    score_pp = jnp.einsum("qhd,khd->hqk", query_p, keys_p, preferred_element_type=F32)
    score_cp = jnp.einsum("nqhd,khd->hnqk", query_c, keys_p, preferred_element_type=F32)
    score_cc = jnp.einsum("nqhd,nkhd->hnqk", query_c, keys_c, preferred_element_type=F32)
    score_pp = jnp.where(rows[None, :] <= rows[:, None], score_pp, NEG)
    score_cp = jnp.where((rows[None, None, :] < offsets[:, None, None])[None], score_cp, NEG)
    score_cc = jnp.where(inner[None, :] <= inner[:, None], score_cc, NEG)
    return (score_pp, score_cp, score_cc)


def attend_forward(q_all, k_all, v_all, offsets):
    score_pp, score_cp, score_cc = score_blocks(q_all, k_all, offsets)
    vals_p, vals_c = split_group(v_all)
    top_p = jnp.max(score_pp, axis=-1, keepdims=True)
    expo_pp = jnp.exp(score_pp - top_p)
    total_p = jnp.sum(expo_pp, axis=-1, keepdims=True)
    top_c = jnp.maximum(
        jnp.max(score_cp, axis=-1, keepdims=True), jnp.max(score_cc, axis=-1, keepdims=True)
    )
    expo_cp = jnp.exp(score_cp - top_c)
    expo_cc = jnp.exp(score_cc - top_c)
    total_c = jnp.sum(expo_cp, axis=-1, keepdims=True) + jnp.sum(expo_cc, axis=-1, keepdims=True)
    prob_pp = (expo_pp / total_p).astype(BF16)
    prob_cp = (expo_cp / total_c).astype(BF16)
    prob_cc = (expo_cc / total_c).astype(BF16)
    out_p = jnp.einsum("hqk,khd->qhd", prob_pp, vals_p, preferred_element_type=F32)
    out_c = jnp.einsum("hnqk,khd->nqhd", prob_cp, vals_p, preferred_element_type=F32)
    out_c = out_c + jnp.einsum("hnqk,nkhd->nqhd", prob_cc, vals_c, preferred_element_type=F32)
    return (
        join_group(out_p, out_c),
        (top_p + jnp.log(total_p))[..., 0],
        (top_c + jnp.log(total_c))[..., 0],
    )


def attend_backward(q_all, k_all, v_all, offsets, lse_prompt, lse_cont, grad_out):
    score_pp, score_cp, score_cc = score_blocks(q_all, k_all, offsets)
    query_p, query_c = split_group(q_all)
    keys_p, keys_c = split_group(k_all)
    vals_p, vals_c = split_group(v_all)
    grad_p, grad_c = split_group(grad_out)
    prob_pp = jnp.exp(score_pp - lse_prompt[..., None])
    prob_cp = jnp.exp(score_cp - lse_cont[..., None])
    prob_cc = jnp.exp(score_cc - lse_cont[..., None])
    back_pp = jnp.einsum("qhd,khd->hqk", grad_p, vals_p, preferred_element_type=F32)
    back_cp = jnp.einsum("nqhd,khd->hnqk", grad_c, vals_p, preferred_element_type=F32)
    back_cc = jnp.einsum("nqhd,nkhd->hnqk", grad_c, vals_c, preferred_element_type=F32)
    low_pp = prob_pp.astype(BF16)
    low_cp = prob_cp.astype(BF16)
    low_cc = prob_cc.astype(BF16)
    value_p = jnp.einsum("hqk,qhd->khd", low_pp, grad_p, preferred_element_type=F32)
    value_p = value_p + jnp.einsum("hnqk,nqhd->khd", low_cp, grad_c, preferred_element_type=F32)
    value_c = jnp.einsum("hnqk,nqhd->nkhd", low_cc, grad_c, preferred_element_type=F32)
    total_p = jnp.sum(prob_pp * back_pp, axis=-1, keepdims=True)
    total_c = jnp.sum(prob_cp * back_cp, axis=-1, keepdims=True) + jnp.sum(
        prob_cc * back_cc, axis=-1, keepdims=True
    )
    soft_pp = (prob_pp * (back_pp - total_p)).astype(BF16)
    soft_cp = (prob_cp * (back_cp - total_c)).astype(BF16)
    soft_cc = (prob_cc * (back_cc - total_c)).astype(BF16)
    query_gp = jnp.einsum("hqk,khd->qhd", soft_pp, keys_p, preferred_element_type=F32)
    query_gc = jnp.einsum("hnqk,khd->nqhd", soft_cp, keys_p, preferred_element_type=F32)
    query_gc = query_gc + jnp.einsum(
        "hnqk,nkhd->nqhd", soft_cc, keys_c, preferred_element_type=F32
    )
    key_gp = jnp.einsum("hqk,qhd->khd", soft_pp, query_p, preferred_element_type=F32)
    key_gp = key_gp + jnp.einsum("hnqk,nqhd->khd", soft_cp, query_c, preferred_element_type=F32)
    key_gc = jnp.einsum("hnqk,nqhd->nkhd", soft_cc, query_c, preferred_element_type=F32)
    return (
        join_group(query_gp, query_gc),
        join_group(key_gp, key_gc),
        join_group(value_p, value_c),
    )


def silu_slope(pre):
    sigma = jax.nn.sigmoid(pre)
    return sigma * (1.0 + pre * (1.0 - sigma))


def on_device(
    inputs,
    input_weight,
    output_weight,
    up_weight,
    down_weight,
    attend_gain,
    feed_gain,
    query_gain,
    branch_points,
    cotangent,
):
    tok, half = inputs.shape
    sub = tok // 2
    n_h = lax.axis_size("h")
    n_z = 2 * n_h
    n_data = lax.axis_size("D")
    ik, ih, il, iy, ix = (lax.axis_index(a) for a in "khlyx")
    iz = ih * 2 + il
    width = 2 * half
    hb = input_weight.shape[2]
    per = n_z // 4
    pair = per * hb
    head_dim = query_gain.shape[0]
    heads = pair // head_dim
    scale = query_gain / math.sqrt(head_dim)

    x_own = swap(inputs)
    x_x = xch(x_own, "x")
    x_y = xch(x_own, "y")
    d_top = xch(x_x[:sub], "y")
    d_bot = xch(x_y[sub:], "x")
    x_d = jnp.concatenate([d_top, d_bot])
    near = [[x_own, x_x], [x_y, x_d]]
    far = [[xch(a, "k") for a in r] for r in near]
    rel = jnp.stack(
        [jnp.concatenate(r, axis=1) for r in near + far]
    )
    group_in = place([((ik ^ (j // 2)) * 2 + (iy ^ (j % 2)), rel[j]) for j in range(4)], 4)
    group_in = group_in.reshape(GROUP_LEN, width).astype(F32)

    w_own = input_weight.reshape(half, 3 * hb)
    arrived = [w_own]
    core_of = [(z // per) % 2 for z in range(n_z)]
    for delta in range(1, n_z):
        pairs = [
            (core_of[z] * n_z + z, core_of[z] * n_z + (z ^ delta)) for z in range(n_z)
        ]
        arrived.append(lax.ppermute(w_own, ("k", "h", "l"), pairs))
    arrived = jnp.stack(arrived)

    def quarter(column):
        first = (2 * column + ik) * per
        return jnp.stack([pick(arrived, (first + i) ^ iz) for i in range(per)])

    w_keep = quarter(ix)
    w_other = xch(quarter(ix ^ 1), "x")
    w_qkv = jnp.stack([w_keep, w_other]).reshape(2, per, half, 3, hb)
    w_qkv = w_qkv.transpose(0, 2, 3, 1, 4).reshape(width, 3 * pair)

    def both(gain):
        return jnp.concatenate([gain, xch(gain, "x")])

    gain_a, gain_f = both(attend_gain), both(feed_gain)

    points = lax.all_gather(branch_points, "x", axis=0, tiled=True)
    points = swap(pick(points, ih))

    cot = swap(cotangent)
    cot_rows = cot.reshape(2, sub, half)
    g_own = jnp.concatenate([pick(cot_rows, ix), xch(pick(cot_rows, ix ^ 1), "x")], axis=1)
    g_own_low = g_own
    resid = jnp.concatenate(
        [pick(x_own.reshape(2, sub, half), ix), pick(x_x.reshape(2, sub, half), ix)], axis=1
    ).astype(F32)

    stack3 = jnp.stack([output_weight, up_weight.T, down_weight])
    hh = hb // 2
    mine = pick(stack3.reshape(3, 2, hh, half), ik, 1)
    zs = [mine] + [
        lax.ppermute(mine, ("h", "l"), [(z, z ^ delta) for z in range(n_z)])
        for delta in range(1, n_z)
    ]
    zpack = place([(iz ^ d, a) for d, a in enumerate(zs)], n_z)
    p_x = xch(zpack, "x")
    p_y = xch(zpack, "y")
    cut = n_z // 2
    p_d = jnp.concatenate([xch(p_x[:cut], "y"), xch(p_y[cut:], "x")])
    near3 = [[zpack, p_x], [p_y, p_d]]
    far3 = [[xch(a, "k") for a in r] for r in near3]
    whole = place(
        [
            ((iy ^ dy) * 2 + (ik ^ dk), jnp.stack(src[dy]))
            for dk, src in enumerate((near3, far3))
            for dy in range(2)
        ],
        4,
    )
    whole = whole.reshape(2, 2, 2, n_z, 3, hh, half).transpose(4, 3, 0, 1, 5, 2, 6)
    w_out, w_up, w_down = whole.reshape(3, n_z * 2 * hb, width)

    inv = lax.rsqrt(jnp.mean(group_in * group_in, axis=1, keepdims=True) + EPS)
    normed = (group_in * inv * gain_a).astype(BF16)
    qkv = dot(normed, w_qkv, 1, 0).reshape(GROUP_LEN, 3, heads, head_dim)
    q_raw = qkv[:, 0]
    q_low = (q_raw * scale).astype(BF16)
    k_low = qkv[:, 1].astype(BF16)
    v_low = qkv[:, 2].astype(BF16)
    attended, lse_p, lse_c = attend_forward(q_low, k_low, v_low, points)
    att_t = attended.astype(BF16).reshape(8, sub, pair).transpose(0, 2, 1)
    plane = ("k", "y", "x")
    att8 = lax.all_to_all(att_t, plane, 0, 0, tiled=True)
    att_own = att8.reshape(2, 2, 2, per, hb, sub).transpose(2, 0, 3, 1, 4, 5)
    att_own = att_own.reshape(width, sub)

    attn_branch = dot(att_own, w_out, 0, 0)
    hidden = resid + attn_branch
    inv_two = lax.rsqrt(jnp.mean(hidden * hidden, axis=1, keepdims=True) + EPS)
    unit_two = hidden * inv_two
    normed_two = (unit_two * gain_f).astype(BF16)
    pre = dot(normed_two, w_up, 1, 1)
    act = jax.nn.silu(pre).astype(BF16)
    feed = dot(act, w_down, 1, 0)
    stream = hidden + feed
    stats = jnp.sqrt(
        jnp.stack([jnp.mean(a * a, axis=1) for a in (attn_branch, feed, stream)])
    )
    act_grad = dot(g_own_low, w_down, 1, 1)
    pre_grad = (act_grad * silu_slope(pre)).astype(BF16)
    n2_grad = dot(pre_grad, w_up, 1, 0)
    feed_gain_part = jnp.sum(n2_grad * unit_two, axis=0)
    u = n2_grad * gain_f
    hidden_grad = g_own.astype(F32) + inv_two * (
        u - unit_two * jnp.mean(u * unit_two, axis=1, keepdims=True)
    )
    branch_low = hidden_grad.astype(BF16)
    att_grad = dot(w_out, branch_low, 1, 1).astype(BF16)
    att_grad = att_grad.reshape(2, 2, per, 2, hb, sub).transpose(1, 3, 0, 2, 4, 5)
    back8 = lax.all_to_all(att_grad.reshape(8, pair, sub), plane, 0, 0, tiled=True)
    grad_att = back8.transpose(0, 2, 1).reshape(GROUP_LEN, heads, head_dim)

    d_out = dot(att_own, branch_low, 1, 0)
    d_up = dot(pre_grad, normed_two, 0, 0)
    d_down = dot(act, g_own_low, 0, 0)
    part = jnp.stack([d_out, d_up, d_down]).astype(BF16)
    part = part.reshape(3, n_z, 2, 2, hh, 2, half)
    part = part.transpose(3, 2, 5, 1, 0, 4, 6)

    def add(a, b):
        return (a.astype(F32) + b.astype(F32)).astype(BF16)

    part = add(pick(part, ik), xch(pick(part, ik ^ 1), "k"))
    upper, lower = part[:, :, :cut], part[:, :, cut:]
    upper = add(upper[:, 0], xch(upper[:, 1], "x"))
    upper = add(pick(upper, iy), xch(pick(upper, iy ^ 1), "y"))
    lower = add(pick(lower, iy), xch(pick(lower, iy ^ 1), "y"))
    lower = add(lower[0], xch(lower[1], "x"))
    rest = jnp.concatenate([upper, lower])
    total = pick(rest, iz).astype(F32)
    for delta in range(1, n_z):
        got = lax.ppermute(
            pick(rest, iz ^ delta), ("h", "l"), [(z, z ^ delta) for z in range(n_z)]
        )
        total = total + got.astype(F32)
    total = total.astype(BF16)
    sum3 = place([(ik, total), (ik ^ 1, xch(total, "k"))], 2)
    sum3 = sum3.transpose(1, 0, 2, 3).reshape(3, hb, half).astype(F32)
    if n_data > 1:
        sum3 = lax.psum(sum3, "D")
    output_weight_grad, up_weight_grad, down_weight_grad = sum3[0], sum3[1].T, sum3[2]

    q_grad, k_grad, v_grad = attend_backward(
        q_low, k_low, v_low, points, lse_p, lse_c, grad_att
    )
    q_gain_part = jnp.sum(q_grad * q_raw, axis=(0, 1)) / math.sqrt(head_dim)
    qkv_grad = jnp.stack([q_grad * scale, k_grad, v_grad], axis=1)
    qkv_grad = qkv_grad.astype(BF16).reshape(GROUP_LEN, 3 * pair)

    dx = dot(qkv_grad, w_qkv, 1, 1).astype(BF16)
    dx = dx.reshape(2, 2, 2, sub, 2, half)
    dx = add(pick(dx, ik), xch(pick(dx, ik ^ 1), "k"))
    top, bot = dx[:, 0], dx[:, 1]
    top = add(top[:, :, 0], xch(top[:, :, 1], "x"))
    top = pick(top, iy).astype(F32) + xch(pick(top, iy ^ 1), "y").astype(F32)
    bot = add(pick(bot, iy), xch(pick(bot, iy ^ 1), "y"))
    bot = bot[:, 0].astype(F32) + xch(bot[:, 1], "x").astype(F32)
    n1_grad = jnp.concatenate([top, bot])

    dw = dot(normed, qkv_grad, 0, 0).astype(BF16)
    dw = dw.reshape(2, half, 3, per, hb).transpose(0, 3, 1, 2, 4).reshape(2, per, half, 3 * hb)
    dw_keep, dw_got = dw[0], xch(dw[1], "x")
    first = (2 * ix + ik) * per
    first_got = (2 * (ix ^ 1) + ik) * per
    pieces = [((first + i) ^ iz, dw_keep[i]) for i in range(per)]
    pieces += [((first_got + i) ^ iz, dw_got[i]) for i in range(per)]
    held = place(pieces, n_z)
    dw_sum = held[0].astype(F32)
    for delta in range(1, n_z):
        pairs = [
            (core_of[z] * n_z + (z ^ delta), core_of[z] * n_z + z) for z in range(n_z)
        ]
        dw_sum = dw_sum + lax.ppermute(held[delta], ("k", "h", "l"), pairs).astype(F32)
    dw_low = dw_sum.astype(BF16)
    dw_far = xch(dw_low, "k")
    dw_low = jnp.where((iz // per) % 2 == ik, dw_low, dw_far).astype(F32)
    if n_data > 1:
        dw_low = lax.psum(dw_low, "D")
    input_weight_grad = dw_low.reshape(half, 3, hb)

    def to_block(full):
        keep, send = full[:, :half], full[:, half:]
        return place([(ix, keep), (ix ^ 1, xch(send, "x"))], 2).reshape(tok, half)

    output = swap(to_block(stream.astype(BF16)))
    hid_block = to_block(hidden_grad)
    stats = swap(place([(ix, stats), (ix ^ 1, xch(stats, "x"))], 2))
    stats = stats.transpose(1, 0, 2).reshape(3, tok)
    own_in = x_own.astype(F32)
    both_in = x_x.astype(F32)
    inv_own = lax.rsqrt(
        (jnp.sum(own_in * own_in, axis=1) + jnp.sum(both_in * both_in, axis=1)) / width + EPS
    )[:, None]
    unit_one = own_in * inv_own
    attend_gain_part = jnp.sum(n1_grad * unit_one, axis=0)
    u1 = n1_grad * attend_gain
    prod = jnp.sum(u1 * unit_one, axis=1)
    prod = prod + xch(prod, "x")
    input_grad = hid_block + inv_own * (u1 - unit_one * (prod / width)[:, None])
    input_grad = swap(input_grad)

    feed_gain_part = feed_gain_part[:half] + xch(feed_gain_part[half:], "x")
    q_gain_pad = jnp.pad(q_gain_part + xch(q_gain_part, "x"), (0, 128 - head_dim))
    sums = lax.psum(
        jnp.concatenate([attend_gain_part, feed_gain_part, q_gain_pad]),
        ("D", "k", "h", "l", "y"),
    )
    return (
        output,
        input_grad,
        input_weight_grad,
        output_weight_grad,
        up_weight_grad,
        down_weight_grad,
        sums[:half],
        sums[half:width],
        sums[width : width + head_dim],
        stats,
    )


def solution(mesh):
    dp, row, col = (mesh.shape[a] for a in ("dp", "row", "col"))
    fine = Mesh(mesh.devices.reshape(dp // 2, 2, row // 4, 2, 2, col), tuple("Dkhlyx"))
    tokens, rows, data = tuple("Dkhly"), tuple("hly"), tuple("Dkx")
    in_specs = (
        P(tokens, "x"),
        P("x", None, rows),
        P(rows, "x"),
        P("x", rows),
        P(rows, "x"),
        P("x"),
        P("x"),
        P(),
        P(data, None),
        P(tokens, "x"),
    )
    out_specs = (
        P(tokens, "x"),
        P(tokens, "x"),
        P("x", None, rows),
        P(rows, "x"),
        P("x", rows),
        P(rows, "x"),
        P("x"),
        P("x"),
        P(),
        P(None, tokens),
    )
    return jax.shard_map(
        on_device, mesh=fine, in_specs=in_specs, out_specs=out_specs, check_vma=False
    )
```
